32 devices in a mesh: mp: 4 (over y, core), latent: 8 (over z, x).
Axes of the slice: x: 2, y: 2, z: 4, core: 2. Of those that a mesh axis runs over, the one named last changes fastest.
Arguments:
- resid_clean: bfloat16 [128, 4608], P(('mp', 'latent')), may hold values from -6 to 6
- resid_corrupt: bfloat16 [128, 4608], P(('mp', 'latent')), may hold values from -6 to 6
- answer_ids: int32 [128, 2], replicated, may hold values from 0 to 127, all different within a row
- unembed: bfloat16 [128, 4608], replicated, may hold values from -1.5 to 1.5
- pre_gain: float32 [4608], replicated, may hold values from 0.25 to 1.75
- post_gain: float32 [4608], replicated, may hold values from 0.25 to 1.75
- final_gain: float32 [4608], replicated, may hold values from 0.25 to 1.75
- w_gate: bfloat16 [4608, 36864], P(None, ('mp', 'latent')), may hold values from -0.09375 to 0.09375
- w_up: bfloat16 [4608, 36864], P(None, ('mp', 'latent')), may hold values from -0.09375 to 0.09375
- w_down: bfloat16 [36864, 4608], P(('mp', 'latent')), may hold values from -0.03125 to 0.03125
- w_enc: bfloat16 [4608, 65536], P(None, ('mp', 'latent')), may hold values from -0.09375 to 0.09375
- b_enc: float32 [65536], P(('mp', 'latent')), may hold values from -3 to 3
- w_dec: bfloat16 [65536, 4608], P(('mp', 'latent')), may hold values from -0.09375 to 0.09375
Outputs:
- attribution: float32 [1, 65536], P(None, ('mp', 'latent'))
The draws below stay inside these ranges and needn't reach their ends.
Inputs may be any that keep to these rules, and one draw needn't show every extreme that they name: `answer_ids`: the two indices of a token differ.
All inputs are finite; a program needn't handle non-finite values.
Results may differ from the reference program's by a relative error of at most 0.0056.
Values may be sent and summed in bfloat16 or wider, within the bound.
A program may use at most 128 MiB of HBM per device.

```python
import jax
import jax.numpy as jnp
from jax import lax

D = 4608
FF = 36864
LATENTS = 65536
CANDS = 128
SEQ = 128
PAIRS = 1
TOK = 128


def block_levels(stream_key, extent, cuts, low, largest):
    def one(position, parts):
        heights = jax.random.uniform(jax.random.fold_in(jax.random.fold_in(stream_key, 6), position), (parts,), jnp.float32, low / len(cuts), largest / len(cuts))
        return jnp.repeat(jnp.exp(heights), extent[position] // parts).reshape((-1,) + (1,) * (len(extent) - position - 1))

    gain = one(*cuts[0])
    for cut in cuts[1:]:
        gain = gain * one(*cut)
    return gain


def distinct(own_key, rows, number_of, top, lift):
    ranking = jax.random.permutation(jax.random.fold_in(own_key, 1), number_of)
    boost = ranking
    for power in range(3):
        boost = boost * boost // number_of
    boost = boost * lift // number_of
    chance = jax.random.randint(jax.random.fold_in(own_key, 2), (rows, number_of), 0, 4096) + boost
    sure = jax.random.permutation(jax.random.fold_in(own_key, 3), rows)[jnp.arange(number_of) % rows]
    chance = jnp.where(jnp.arange(rows)[:, None] == sure[None, :], 1 << 14, chance)
    score = chance * number_of + jnp.arange(number_of)
    return lax.top_k(score.astype(jnp.int32), top)[1].astype(jnp.int32)


def noise(own_key, extent, spread, bound, split=(), kind=jnp.bfloat16):
    level = block_levels(own_key, extent, split, -0.22, 0.18) if split else 1.0
    values = jax.random.normal(own_key, extent, jnp.float32) * spread * level
    return jnp.minimum(jnp.maximum(values, -bound), bound).astype(kind)


def setup_inputs(seed: int = 0) -> dict:
    keys = jax.random.split(jax.random.key(seed), 14)
    resid_clean = noise(keys[0], (TOK, D), 1.0, 6.0, ((0, 32),))
    resid_corrupt = noise(keys[1], (TOK, D), 1.0, 6.0, ((0, 32),))
    answer_ids = distinct(keys[2], TOK, CANDS, 2, 0)
    unembed = noise(keys[3], (CANDS, D), 0.25, 1.5)
    pre_gain = jnp.clip(1.0 + 0.15 * jax.random.normal(keys[4], (D,), jnp.float32), 0.25, 1.75)
    post_gain = jnp.clip(1.0 + 0.15 * jax.random.normal(keys[5], (D,), jnp.float32), 0.25, 1.75)
    final_gain = jnp.clip(1.0 + 0.15 * jax.random.normal(keys[6], (D,), jnp.float32), 0.25, 1.75)
    w_gate = noise(keys[7], (D, FF), D ** -0.5, 0.09375, ((1, 32),))
    w_up = noise(keys[8], (D, FF), D ** -0.5, 0.09375, ((1, 32),))
    w_down = noise(keys[9], (FF, D), FF ** -0.5, 0.03125, ((0, 32),))
    w_enc = noise(keys[10], (D, LATENTS), D ** -0.5, 0.09375, ((1, 32),))
    b_enc = noise(keys[11], (LATENTS,), 0.5, 3.0, ((0, 32),), jnp.float32)
    w_dec = noise(keys[12], (LATENTS, D), D ** -0.5, 0.09375, ((0, 32),))
    return {"resid_clean": resid_clean, "resid_corrupt": resid_corrupt, "answer_ids": answer_ids, "unembed": unembed, "pre_gain": pre_gain, "post_gain": post_gain, "final_gain": final_gain, "w_gate": w_gate, "w_up": w_up, "w_down": w_down, "w_enc": w_enc, "b_enc": b_enc, "w_dec": w_dec}


epsilon = 1e-06
gelu_scale = 0.7978845608028654
gelu_cubic = 0.044715

def gelu_tanh(value):
    return 0.5 * value * (1.0 + jnp.tanh(gelu_scale * (value + gelu_cubic * value * value * value)))

def gelu_slope(value):
    inner = jnp.tanh(gelu_scale * (value + gelu_cubic * value * value * value))
    return 0.5 * (1.0 + inner) + 0.5 * value * (1.0 - inner * inner) * gelu_scale * (1.0 + 3.0 * gelu_cubic * value * value)

def contract_last(left, right):
    return lax.dot_general(left, right, (((1,), (1,)), ((), ())), preferred_element_type=jnp.float32)

def output_grads(stream, mlp_out, answers, unembed, post_gain, final_gain):
    inv_post = lax.rsqrt(lax.optimization_barrier(jnp.mean(mlp_out * mlp_out, axis=-1, keepdims=True)) + epsilon)
    output = stream + mlp_out * inv_post * post_gain
    inv_final = lax.rsqrt(lax.optimization_barrier(jnp.mean(output * output, axis=-1, keepdims=True)) + epsilon)
    candidate = lax.broadcasted_iota(jnp.int32, (answers.shape[0], unembed.shape[0]), 1)
    selector = ((candidate == answers[:, 0:1]).astype(jnp.float32) - (candidate == answers[:, 1:2]).astype(jnp.float32)).astype(jnp.bfloat16)
    direction = jnp.dot(selector, unembed, preferred_element_type=jnp.float32)
    weighted = final_gain * direction
    grad_output = inv_final * weighted - output * (inv_final * inv_final * inv_final) * lax.optimization_barrier(jnp.mean(weighted * output, axis=-1, keepdims=True))
    post_grad = post_gain * grad_output
    grad_mlp = (inv_post * post_grad - mlp_out * (inv_post * inv_post * inv_post) * lax.optimization_barrier(jnp.mean(post_grad * mlp_out, axis=-1, keepdims=True))).astype(jnp.bfloat16)
    return (grad_output, grad_mlp)

def reference(resid_clean, resid_corrupt, answer_ids, unembed, pre_gain, post_gain, final_gain, w_gate, w_up, w_down, w_enc, b_enc, w_dec):
    stream = resid_clean.astype(jnp.float32)
    inv_pre = lax.rsqrt(lax.optimization_barrier(jnp.mean(stream * stream, axis=-1, keepdims=True)) + epsilon)
    normed = (stream * inv_pre * pre_gain).astype(jnp.bfloat16)
    gate_pre = jnp.dot(normed, w_gate, preferred_element_type=jnp.float32)
    up_proj = jnp.dot(normed, w_up, preferred_element_type=jnp.float32)
    activated = gelu_tanh(gate_pre)
    hidden = (activated * up_proj).astype(jnp.bfloat16)
    mlp_out = jnp.dot(hidden, w_down, preferred_element_type=jnp.float32)
    grad_output, grad_mlp = output_grads(stream, mlp_out, answer_ids, unembed, post_gain, final_gain)
    grad_hidden = contract_last(grad_mlp, w_down)
    grad_gate = (grad_hidden * up_proj * gelu_slope(gate_pre)).astype(jnp.bfloat16)
    grad_up = (grad_hidden * activated).astype(jnp.bfloat16)
    grad_normed = contract_last(grad_gate, w_gate) + contract_last(grad_up, w_up)
    pre_grad = pre_gain * grad_normed
    grad_stream = (grad_output + inv_pre * pre_grad - stream * (inv_pre * inv_pre * inv_pre) * lax.optimization_barrier(jnp.mean(pre_grad * stream, axis=-1, keepdims=True))).astype(jnp.bfloat16)
    clean_code = jax.nn.relu(jnp.dot(resid_clean, w_enc, preferred_element_type=jnp.float32) + b_enc)
    corrupt_code = jax.nn.relu(jnp.dot(resid_corrupt, w_enc, preferred_element_type=jnp.float32) + b_enc)
    change = clean_code - corrupt_code
    projected = contract_last(grad_stream, w_dec)
    product = change * projected
    return lax.optimization_barrier(jnp.sum(product.reshape(PAIRS, SEQ, LATENTS), axis=1))
```

```python
import functools

import jax
import jax.numpy as jnp
from jax import lax
from jax.experimental import pallas as pl
from jax.experimental.pallas import tpu as pltpu
from jax.sharding import PartitionSpec as P

SEQ = 128


epsilon = 1e-06
gelu_scale = 0.7978845608028654
gelu_cubic = 0.044715


def gelu_tanh(value):
    return 0.5 * value * (1.0 + jnp.tanh(gelu_scale * (value + gelu_cubic * value * value * value)))


def gelu_slope(value):
    inner = jnp.tanh(gelu_scale * (value + gelu_cubic * value * value * value))
    return 0.5 * (1.0 + inner) + 0.5 * value * (1.0 - inner * inner) * gelu_scale * (
        1.0 + 3.0 * gelu_cubic * value * value
    )


def contract_last(left, right):
    return lax.dot_general(
        left, right, (((1,), (1,)), ((), ())), preferred_element_type=jnp.float32
    )


def output_grads(stream, mlp_out, answers, unembed, post_gain, final_gain):
    inv_post = lax.rsqrt(jnp.mean(mlp_out * mlp_out, axis=-1, keepdims=True) + epsilon)
    output = stream + mlp_out * inv_post * post_gain
    inv_final = lax.rsqrt(jnp.mean(output * output, axis=-1, keepdims=True) + epsilon)
    candidate = lax.broadcasted_iota(jnp.int32, (answers.shape[0], unembed.shape[0]), 1)
    selector = (
        (candidate == answers[:, 0:1]).astype(jnp.float32)
        - (candidate == answers[:, 1:2]).astype(jnp.float32)
    ).astype(jnp.bfloat16)
    direction = jnp.dot(selector, unembed, preferred_element_type=jnp.float32)
    weighted = final_gain * direction
    grad_output = inv_final * weighted - output * (inv_final * inv_final * inv_final) * jnp.mean(
        weighted * output, axis=-1, keepdims=True
    )
    post_grad = post_gain * grad_output
    grad_mlp = (
        inv_post * post_grad
        - mlp_out
        * (inv_post * inv_post * inv_post)
        * jnp.mean(post_grad * mlp_out, axis=-1, keepdims=True)
    ).astype(jnp.bfloat16)
    return (grad_output, grad_mlp)


def local(
    resid_clean,
    resid_corrupt,
    answer_ids,
    unembed,
    pre_gain,
    post_gain,
    final_gain,
    w_gate,
    w_up,
    w_down,
    w_enc,
    b_enc,
    w_dec,
):
    own_rows = resid_clean.shape[0]
    clean_all, corrupt_all = (
        lax.all_gather(resid_clean, ("mp", "latent"), axis=0, tiled=True),
        lax.all_gather(resid_corrupt, ("mp", "latent"), axis=0, tiled=True),
    )
    total_rows = clean_all.shape[0]
    offset = lax.axis_index(("mp", "latent")) * own_rows
    stream = clean_all.astype(jnp.float32)
    inv_pre = lax.rsqrt(jnp.mean(stream * stream, axis=-1, keepdims=True) + epsilon)
    normed = (stream * inv_pre * pre_gain).astype(jnp.bfloat16)
    gate_pre = jnp.dot(normed, w_gate, preferred_element_type=jnp.float32)
    up_proj = jnp.dot(normed, w_up, preferred_element_type=jnp.float32)
    activated = gelu_tanh(gate_pre)
    hidden = (activated * up_proj).astype(jnp.bfloat16)
    stream_rows = lax.dynamic_slice_in_dim(stream, offset, own_rows, 0)
    inv_rows = lax.dynamic_slice_in_dim(inv_pre, offset, own_rows, 0)
    mlp_out = lax.psum(
        jnp.dot(hidden, w_down, preferred_element_type=jnp.float32), ("mp", "latent")
    )
    grad_output, grad_mlp = output_grads(
        stream, mlp_out, answer_ids, unembed, post_gain, final_gain
    )
    grad_hidden = contract_last(grad_mlp, w_down)
    grad_rows_out = lax.dynamic_slice_in_dim(grad_output, offset, own_rows, 0)
    grad_gate = (grad_hidden * up_proj * gelu_slope(gate_pre)).astype(jnp.bfloat16)
    grad_up = (grad_hidden * activated).astype(jnp.bfloat16)
    grad_normed = lax.psum_scatter(
        contract_last(grad_gate, w_gate) + contract_last(grad_up, w_up),
        ("mp", "latent"),
        scatter_dimension=0,
        tiled=True,
    )
    pre_grad = pre_gain * grad_normed
    grad_stream = (
        grad_rows_out
        + inv_rows * pre_grad
        - stream_rows
        * (inv_rows * inv_rows * inv_rows)
        * jnp.mean(pre_grad * stream_rows, axis=-1, keepdims=True)
    ).astype(jnp.bfloat16)
    clean_code = jax.nn.relu(jnp.dot(clean_all, w_enc, preferred_element_type=jnp.float32) + b_enc)
    corrupt_code = jax.nn.relu(
        jnp.dot(corrupt_all, w_enc, preferred_element_type=jnp.float32) + b_enc
    )
    change = clean_code - corrupt_code
    projected = contract_last(
        lax.all_gather(grad_stream, ("mp", "latent"), axis=0, tiled=True), w_dec
    )
    product = change * projected
    return jnp.sum(product.reshape(total_rows // SEQ, SEQ, product.shape[1]), axis=1)


MESH = pl.DeviceIdType.MESH
BF = jnp.bfloat16
F32 = jnp.float32


PARTS = 3
LANES = 128


class Place:
    def __init__(self, depth):
        self.depth = depth
        self.mp = lax.axis_index("mp")
        self.lat = lax.axis_index("latent")
        self.c, self.y = self.mp % 2, self.mp // 2
        self.x, self.z = self.lat % 2, self.lat // 2
        mp_y, lat_x = (1 - self.y) * 2 + self.c, self.z * 2 + 1 - self.x
        self.core_peer = (self.y * 2 + 1 - self.c, self.lat)
        self.flat_peers = [(self.mp, lat_x), (mp_y, self.lat), (mp_y, lat_x)]
        x, y = self.x, self.y
        self.flat_blocks = [y * 2 + 1 - x, (1 - y) * 2 + x, (1 - y) * 2 + 1 - x]
        self.block = y * 2 + x

    def z_peer(self, step):
        return (self.mp, ((self.z + step) % self.depth) * 2 + self.x)

    def peers(self):
        return [self.core_peer] + self.flat_peers + [self.z_peer(step) for step in range(1, self.depth)]

    def greet(self):
        barrier = pltpu.get_barrier_semaphore()
        for peer in self.peers():
            pl.semaphore_signal(barrier, inc=1, device_id=peer, device_id_type=MESH)

    def meet(self):
        pl.semaphore_wait(pltpu.get_barrier_semaphore(), len(self.peers()))


class Wires:
    def __init__(self, send, recv):
        self.send, self.recv, self.used = send, recv, 0

    def start(self, src, dst, peer):
        i = self.used
        self.used += 1
        copy = pltpu.make_async_remote_copy(
            src_ref=src, dst_ref=dst, send_sem=self.send.at[i], recv_sem=self.recv.at[i],
            device_id=peer, device_id_type=MESH,
        )
        copy.start()
        return copy


def finish(copies):
    for copy in copies:
        copy.wait()


def rows16(start):
    return pl.ds(pl.multiple_of(start, 16), 16)


def rows64(start):
    return pl.ds(pl.multiple_of(start, 64), 64)


def fold(value, depth, row=0):
    width = value.shape[1] // depth
    tokens = 16 // depth
    return jnp.concatenate(
        [value[row : row + tokens, s * width : (s + 1) * width] for s in range(depth)], axis=0
    )


def unfold(blocks, depth):
    tokens = 16 // depth
    return [
        jnp.concatenate([block[s * tokens : (s + 1) * tokens] for block in blocks], axis=0) for s in range(depth)
    ]


class Gather:
    def __init__(self, at, wires, zin, buf, base):
        self.at, self.wires, self.zin, self.buf, self.base = at, wires, zin, buf, base
        self.fine = zin.shape[2] // PARTS
        self.wide = buf.shape[1] // PARTS

    def start(self):
        at, fine = self.at, self.fine
        self.deep = []
        for k in range(PARTS):
            spot = self.zin.at[at.z, :, pl.ds(k * fine, fine)]
            self.deep.append([self.wires.start(spot, spot, at.z_peer(s)) for s in range(1, at.depth)])
        self.flat, self.core = [], []

    def relay(self, k):
        at, fine, wide = self.at, self.fine, self.wide
        finish(self.deep[k])
        blocks = [self.zin[z, :, k * fine : (k + 1) * fine].astype(F32) for z in range(at.depth)]
        mine = rows16(self.base + at.c * 64 + at.block * 16)
        for s, value in enumerate(unfold(blocks, at.depth)):
            self.buf[mine, k * wide + s * fine : k * wide + (s + 1) * fine] = value.astype(BF)
        spot = self.buf.at[mine, pl.ds(k * wide, wide)]
        self.flat.append([self.wires.start(spot, spot, peer) for peer in at.flat_peers])

    def across(self, k):
        finish(self.flat[k])
        spot = self.buf.at[rows64(self.base + self.at.c * 64), pl.ds(k * self.wide, self.wide)]
        self.core.append(self.wires.start(spot, spot, self.at.core_peer))

    def close(self, k):
        finish([self.core[k]])


class Scatter:
    def __init__(self, at, wires, part, bufs, total):
        self.at, self.wires, self.part, self.total = at, wires, part, total
        self.rc, self.s1, self.rf, self.kept, self.sent, self.rz = bufs
        self.wide = part.shape[1] // PARTS
        self.fine = total.shape[1] // PARTS
        self.core, self.flat, self.deep = [], [], []

    def start(self, k):
        span = pl.ds(k * self.wide, self.wide)
        peer = rows64((1 - self.at.c) * 64)
        self.core.append(self.wires.start(self.part.at[peer, span], self.rc.at[:, span], self.at.core_peer))

    def pair(self, k):
        at, wide = self.at, self.wide
        span = pl.ds(k * wide, wide)
        finish([self.core[k]])
        for b in range(4):
            rows = rows16(at.c * 64 + b * 16)
            here = slice(b * 16, b * 16 + 16)
            self.s1[here, span] = (self.part[rows, span].astype(F32) + self.rc[here, span].astype(F32)).astype(BF)
        self.flat.append([
            self.wires.start(self.s1.at[rows16(block * 16), span], self.rf.at[i, :, span], peer)
            for i, (block, peer) in enumerate(zip(at.flat_blocks, at.flat_peers))
        ])

    def settle(self, k):
        at, wide, fine = self.at, self.wide, self.fine
        span = pl.ds(k * wide, wide)
        slot = pl.ds(k * fine, fine)
        finish(self.flat[k])
        value = self.s1[rows16(at.block * 16), span].astype(F32)
        for i in range(3):
            value = value + self.rf[i, :, span].astype(F32)
        for z in range(at.depth):
            piece = fold(value, at.depth, z * (16 // at.depth))
            self.kept[z, :, slot] = piece
            self.sent[z, :, slot] = piece.astype(BF)
        self.deep.append([
            self.wires.start(self.sent.at[(at.z + s) % at.depth, :, slot], self.rz.at[s - 1, :, slot], at.z_peer(s))
            for s in range(1, at.depth)
        ])

    def close(self, k):
        slot = pl.ds(k * self.fine, self.fine)
        finish(self.deep[k])
        value = self.kept[self.at.z, :, slot]
        for s in range(1, self.at.depth):
            value = value + self.rz[s - 1, :, slot].astype(F32)
        self.total[:, slot] = value


def scatter_buffers(d, depth):
    width = d // depth
    return [
        pltpu.VMEM((64, d), BF), pltpu.VMEM((64, d), BF), pltpu.VMEM((3, 16, d), BF),
        pltpu.VMEM((depth, 16, width), F32), pltpu.VMEM((depth, 16, width), BF),
        pltpu.VMEM((depth - 1, 16, width), BF),
    ]


def token_sum(value, depth):
    tokens = 16 // depth
    piece = jnp.broadcast_to(jnp.sum(value, axis=-1, keepdims=True), (16, LANES))
    result = piece
    for s in range(1, depth):
        result = result + pltpu.roll(piece, s * tokens, 0)
    return result[:, 0:1]


def whole_kernel(
    depth, clean, corrupt, answers, unembed_hbm, pre_hbm, post_hbm, final_hbm, wg_hbm, wu_hbm, wd_hbm, we_hbm, be_hbm, wl_hbm, out,
    send, recv, load, wgu, wd, we, wl, unembed, pre_gain, post_gain, final_gain, b_enc, zclean, zcorrupt, zgrad, xs, normed, gu, hidden, gcat,
    part, grads, change, projected, total, stream, pre_f, post_f, weighted, kept, *bufs,
):
    d, both = wgu.shape
    units = both // 2
    latents = out.shape[1]
    rows = normed.shape[0]
    wide, fine = d // PARTS, d // depth // PARTS
    own_rows = clean.shape[0]
    tile = we.shape[2]
    first = latents // 2
    count = latents // tile
    loads = [
        pltpu.make_async_copy(wg_hbm, wgu.at[:, 0:units], load.at[0]),
        pltpu.make_async_copy(wu_hbm, wgu.at[:, units:both], load.at[1]),
        pltpu.make_async_copy(wd_hbm, wd, load.at[2]),
        pltpu.make_async_copy(unembed_hbm, unembed, load.at[3]),
        pltpu.make_async_copy(wl_hbm.at[first:latents], wl, load.at[4]),
    ]
    low = pltpu.make_async_copy(wl_hbm.at[0:first], wd.at[0:first], load.at[5])
    gains = (pre_gain, post_gain, final_gain)
    small = [
        pltpu.make_async_copy(source, gains[i].at[0], load.at[8 + i])
        for i, source in enumerate((pre_hbm, post_hbm, final_hbm))
    ] + [pltpu.make_async_copy(be_hbm, b_enc.at[0], load.at[11])]

    def piece(p):
        return pltpu.make_async_copy(we_hbm.at[:, p * tile : (p + 1) * tile], we.at[p % 2], load.at[6 + p % 2])

    at = Place(depth)
    at.greet()
    for copy in small:
        copy.start()
    for copy in loads[:4]:
        copy.start()
    clean_rows, corrupt_rows = clean[...].astype(F32), corrupt[...].astype(F32)
    for k in range(PARTS):
        span, slot = slice(k * wide, (k + 1) * wide), slice(k * fine, (k + 1) * fine)
        value = fold(clean_rows[:, span], depth)
        stream[:, slot] = value
        zclean[at.z, :, slot] = value.astype(BF)
        zcorrupt[at.z, :, slot] = fold(corrupt_rows[:, span], depth).astype(BF)
    at.meet()
    wires = Wires(send, recv)
    first_rows = Gather(at, wires, zclean, xs, 0)
    other_rows = Gather(at, wires, zcorrupt, xs, rows)
    first_rows.start()
    finish(small)
    for k in range(PARTS):
        span, slot = slice(k * wide, (k + 1) * wide), slice(k * fine, (k + 1) * fine)
        for i, place in enumerate((pre_f, post_f, weighted)):
            place[:, slot] = fold(jnp.broadcast_to(gains[i][:, span], (own_rows, wide)), depth)
    for k in range(PARTS):
        first_rows.relay(k)
    other_rows.start()
    for k in range(PARTS):
        first_rows.across(k)
        if k == 0:
            piece(0).start()
            piece(1).start()
            loads[4].start()
        other_rows.relay(k)
        if k > 0:
            first_rows.close(k - 1)
    first_rows.close(PARTS - 1)

    @pl.loop(0, rows // 16)
    def _(i):
        span = rows16(i * 16)
        value = xs[span, :].astype(F32)
        inv_pre = lax.rsqrt(jnp.sum(value * value, axis=-1, keepdims=True) * (1.0 / d) + epsilon)
        normed[span, :] = (value * inv_pre * pre_gain[...]).astype(BF)

    loads[0].wait()
    loads[1].wait()
    cuts = [(a, min(a + 256, units)) for a in range(0, units, 256)]
    for n, (a, b) in enumerate(cuts):
        gate = jnp.dot(normed[...], wgu[:, a:b], preferred_element_type=F32)
        lift = jnp.dot(normed[...], wgu[:, units + a : units + b], preferred_element_type=F32)
        gu[:, a:b] = gate
        gu[:, units + a : units + b] = lift
        hidden[:, a:b] = (gelu_tanh(gate) * lift).astype(BF)
        if n == 1:
            other_rows.across(0)
    loads[2].wait()

    def forward(k):
        for a in range(k * wide, (k + 1) * wide, 512):
            part[:, a : a + 512] = jnp.dot(hidden[...], wd[:, a : a + 512], preferred_element_type=F32).astype(BF)

    def backward(k):
        for a in range(k * wide, (k + 1) * wide, 512):
            part[:, a : a + 512] = contract_last(gcat[...], wgu[a : a + 512, :]).astype(BF)

    def aim():
        loads[3].wait()
        base = (at.mp * (2 * depth) + at.lat) * own_rows
        candidate = lax.broadcasted_iota(jnp.int32, (unembed.shape[0], rows), 0)
        selector = (
            jnp.where(candidate == answers[0:1, :], 1.0, 0.0) - jnp.where(candidate == answers[1:2, :], 1.0, 0.0)
        ).astype(BF)
        token = lax.broadcasted_iota(jnp.int32, (rows, 16), 0)
        lane = lax.broadcasted_iota(jnp.int32, (rows, 16), 1)
        pick = jnp.where(token == base + lane % own_rows, 1.0, 0.0).astype(BF)
        chosen = jnp.dot(selector, pick, preferred_element_type=F32).astype(BF)
        for k in range(PARTS):
            value = lax.dot_general(
                chosen, unembed[:, k * wide : (k + 1) * wide], (((0,), (0,)), ((), ())), preferred_element_type=F32
            )
            slot = slice(k * fine, (k + 1) * fine)
            weighted[:, slot] = weighted[:, slot] * fold(value, depth)

    def slopes():
        for a, b in cuts:
            gate, lift = gu[:, a:b], gu[:, units + a : units + b]
            gu[:, a:b] = lift * gelu_slope(gate)
            gu[:, units + a : units + b] = gelu_tanh(gate)

    def encode():
        for p in range(count):
            piece(p).wait()
            span = slice(p * tile, (p + 1) * tile)
            code = jnp.dot(xs[...], we[p % 2], preferred_element_type=F32) + b_enc[:, span]
            code = jnp.maximum(code, 0.0)
            change[:, span] = code[:rows] - code[rows:]
            if p + 2 < count:
                piece(p + 2).start()
            yield

    work = encode()

    def fill(n):
        for _ in range(n):
            next(work, None)

    def scatter(produce, early, plan):
        run = Scatter(at, wires, part, bufs, total)
        for k in range(PARTS):
            produce(k)
            run.start(k)
            if early is not None:
                early(k)
            if k > 0:
                run.pair(k - 1)
        run.pair(PARTS - 1)
        plan(0)
        for k in range(PARTS):
            run.settle(k)
            plan(k + 1)
        for k in range(PARTS):
            run.close(k)

    def gather(zin, use, plan):
        run = Gather(at, wires, zin, grads, 0)
        run.start()
        for k in range(PARTS):
            run.relay(k)
        plan(0)
        for k in range(PARTS):
            run.across(k)
            plan(k + 1)
            run.close(k)
            use(k)

    def early(k):
        if k == 0:
            other_rows.across(1)
            other_rows.close(0)
        elif k == 1:
            other_rows.across(2)
            other_rows.close(1)
        else:
            other_rows.close(2)

    def plan(k):
        if k == 0:
            slopes()
            aim()
            fill(2)
        else:
            fill(1)

    scatter(forward, early, plan)
    m, s, pg, wt = total[...], stream[...], post_f[...], weighted[...]
    mg = m * pg
    mean = lambda value: token_sum(value, depth) * (1.0 / d)
    mm, ss, smg, mgmg, ws, wmg = mean(m * m), mean(s * s), mean(s * mg), mean(mg * mg), mean(wt * s), mean(wt * mg)
    inv_post = lax.rsqrt(mm + epsilon)
    inv_final = lax.rsqrt(ss + 2.0 * inv_post * smg + inv_post * inv_post * mgmg + epsilon)
    output = s + mg * inv_post
    lean = (inv_final * inv_final * inv_final) * (ws + inv_post * wmg)
    grad_output = inv_final * wt - output * lean
    pull = inv_final * wmg - lean * (smg + inv_post * mgmg)
    grad_mlp = inv_post * (pg * grad_output) - m * (inv_post * inv_post * inv_post) * pull
    kept[...] = grad_output
    zgrad[at.z] = grad_mlp.astype(BF)

    def hidden_grad(k):
        span = slice(k * wide, (k + 1) * wide)
        for a, b in cuts:
            value = contract_last(grads[:, span], wd[a:b, span])
            if k > 0:
                value = value + projected[:, a:b]
            if k + 1 < PARTS:
                projected[:, a:b] = value
            else:
                gcat[:, a:b] = (value * gu[:, a:b]).astype(BF)
                gcat[:, units + a : units + b] = (value * gu[:, units + a : units + b]).astype(BF)

    gather(zgrad, hidden_grad, lambda k: fill(1) if k == 0 else None)
    low.start()
    scatter(backward, None, lambda k: fill(1))
    pre_grad = pre_f[...] * total[...]
    s = stream[...]
    inv_pre = lax.rsqrt(mean(s * s) + epsilon)
    lean = (inv_pre * inv_pre * inv_pre) * mean(pre_grad * s)
    zgrad[at.z] = (kept[...] + inv_pre * pre_grad - s * lean).astype(BF)
    fill(count)
    loads[4].wait()
    low.wait()

    def decode(k):
        span = slice(k * wide, (k + 1) * wide)
        step = 512
        for a in range(0, latents, step):
            source = wd if a + step <= first else wl
            base = a % first
            value = contract_last(grads[:, span], source[base : base + step, span])
            if k > 0:
                value = value + projected[:, a : a + step]
            if k + 1 < PARTS:
                projected[:, a : a + step] = value
            else:
                out[:, a : a + step] = jnp.sum(change[:, a : a + step] * value, axis=0, keepdims=True)

    gather(zgrad, decode, lambda k: None)


def staged(
    depth,
    resid_clean,
    resid_corrupt,
    answer_ids,
    unembed,
    pre_gain,
    post_gain,
    final_gain,
    w_gate,
    w_up,
    w_down,
    w_enc,
    b_enc,
    w_dec,
):
    own_rows, d = resid_clean.shape
    width = d // depth
    units = w_gate.shape[1]
    latents = w_enc.shape[1]
    rows = own_rows * depth * 8
    tile = 256
    vmem = pl.BlockSpec(memory_space=pltpu.VMEM)
    hbm = pl.BlockSpec(memory_space=pl.ANY)
    scratch = [
        pltpu.SemaphoreType.DMA((128,)), pltpu.SemaphoreType.DMA((128,)), pltpu.SemaphoreType.DMA((12,)),
        pltpu.VMEM((d, 2 * units), BF), pltpu.VMEM((units, d), BF),
        pltpu.VMEM((2, d, tile), BF), pltpu.VMEM((latents // 2, d), BF), pltpu.VMEM(unembed.shape, BF),
        pltpu.VMEM((1, d), F32), pltpu.VMEM((1, d), F32), pltpu.VMEM((1, d), F32), pltpu.VMEM((1, latents), F32),
        pltpu.VMEM((depth, 16, width), BF), pltpu.VMEM((depth, 16, width), BF), pltpu.VMEM((depth, 16, width), BF),
        pltpu.VMEM((2 * rows, d), BF), pltpu.VMEM((rows, d), BF),
        pltpu.VMEM((rows, 2 * units), F32), pltpu.VMEM((rows, units), BF), pltpu.VMEM((rows, 2 * units), BF),
        pltpu.VMEM((rows, d), BF), pltpu.VMEM((rows, d), BF), pltpu.VMEM((rows, latents), F32),
        pltpu.VMEM((rows, latents), F32),
    ] + [pltpu.VMEM((16, width), F32)] * 6 + scatter_buffers(d, depth)
    return pl.pallas_call(
        functools.partial(whole_kernel, depth),
        out_shape=jax.ShapeDtypeStruct((1, latents), F32),
        in_specs=[vmem] * 3 + [hbm] * 10,
        out_specs=vmem,
        scratch_shapes=scratch,
        compiler_params=pltpu.CompilerParams(
            collective_id=0, has_side_effects=True, vmem_limit_bytes=67043328
        ),
    )(
        resid_clean, resid_corrupt, answer_ids.T, unembed, pre_gain, post_gain, final_gain,
        w_gate, w_up, w_down, w_enc, b_enc, w_dec,
    )


def fits(mesh, own_rows, d, units, latents, candidates):
    depth = mesh.shape["latent"] // 2
    rows = own_rows * mesh.shape["mp"] * mesh.shape["latent"]
    return (
        mesh.shape["mp"] == 4 and depth in (2, 4) and own_rows * depth == 16 and rows == SEQ
        and d % (128 * depth * PARTS) == 0 and d % (512 * PARTS) == 0 and candidates % 128 == 0
        and units % 128 == 0 and latents % 1024 == 0 and latents // 2 <= units
    )


def solution(mesh):
    def chosen(resid_clean, *rest):
        own_rows, d = resid_clean.shape
        if fits(mesh, own_rows, d, rest[6].shape[1], rest[9].shape[1], rest[2].shape[0]):
            return staged(mesh.shape["latent"] // 2, resid_clean, *rest)
        return local(resid_clean, *rest)

    return jax.shard_map(
        chosen,
        mesh=mesh,
        in_specs=(
            P(("mp", "latent"), None),
            P(("mp", "latent"), None),
            P(),
            P(),
            P(),
            P(),
            P(),
            P(None, ("mp", "latent")),
            P(None, ("mp", "latent")),
            P(("mp", "latent"), None),
            P(None, ("mp", "latent")),
            P(("mp", "latent")),
            P(("mp", "latent"), None),
        ),
        out_specs=P(None, ("mp", "latent")),
        check_vma=False,
    )
```

```python
import functools
import itertools

import jax
import jax.numpy as jnp
from jax import lax
from jax.experimental import pallas as pl
from jax.experimental.pallas import tpu as pltpu
from jax.sharding import PartitionSpec as P

SEQ = 128


epsilon = 1e-06
gelu_scale = 0.7978845608028654
gelu_cubic = 0.044715


def gelu_tanh(value):
    return 0.5 * value * (1.0 + jnp.tanh(gelu_scale * (value + gelu_cubic * value * value * value)))


def gelu_slope(value):
    inner = jnp.tanh(gelu_scale * (value + gelu_cubic * value * value * value))
    return 0.5 * (1.0 + inner) + 0.5 * value * (1.0 - inner * inner) * gelu_scale * (
        1.0 + 3.0 * gelu_cubic * value * value
    )


def contract_last(left, right):
    return lax.dot_general(
        left, right, (((1,), (1,)), ((), ())), preferred_element_type=jnp.float32
    )


def output_grads(stream, mlp_out, answers, unembed, post_gain, final_gain):
    inv_post = lax.rsqrt(jnp.mean(mlp_out * mlp_out, axis=-1, keepdims=True) + epsilon)
    output = stream + mlp_out * inv_post * post_gain
    inv_final = lax.rsqrt(jnp.mean(output * output, axis=-1, keepdims=True) + epsilon)
    candidate = lax.broadcasted_iota(jnp.int32, (answers.shape[0], unembed.shape[0]), 1)
    selector = (
        (candidate == answers[:, 0:1]).astype(jnp.float32)
        - (candidate == answers[:, 1:2]).astype(jnp.float32)
    ).astype(jnp.bfloat16)
    direction = jnp.dot(selector, unembed, preferred_element_type=jnp.float32)
    weighted = final_gain * direction
    grad_output = inv_final * weighted - output * (inv_final * inv_final * inv_final) * jnp.mean(
        weighted * output, axis=-1, keepdims=True
    )
    post_grad = post_gain * grad_output
    grad_mlp = (
        inv_post * post_grad
        - mlp_out
        * (inv_post * inv_post * inv_post)
        * jnp.mean(post_grad * mlp_out, axis=-1, keepdims=True)
    ).astype(jnp.bfloat16)
    return (grad_output, grad_mlp)


def local(
    resid_clean,
    resid_corrupt,
    answer_ids,
    unembed,
    pre_gain,
    post_gain,
    final_gain,
    w_gate,
    w_up,
    w_down,
    w_enc,
    b_enc,
    w_dec,
):
    own_rows = resid_clean.shape[0]
    clean_all, corrupt_all = (
        lax.all_gather(resid_clean, ("mp", "latent"), axis=0, tiled=True),
        lax.all_gather(resid_corrupt, ("mp", "latent"), axis=0, tiled=True),
    )
    total_rows = clean_all.shape[0]
    offset = lax.axis_index(("mp", "latent")) * own_rows
    stream = clean_all.astype(jnp.float32)
    inv_pre = lax.rsqrt(jnp.mean(stream * stream, axis=-1, keepdims=True) + epsilon)
    normed = (stream * inv_pre * pre_gain).astype(jnp.bfloat16)
    gate_pre = jnp.dot(normed, w_gate, preferred_element_type=jnp.float32)
    up_proj = jnp.dot(normed, w_up, preferred_element_type=jnp.float32)
    activated = gelu_tanh(gate_pre)
    hidden = (activated * up_proj).astype(jnp.bfloat16)
    stream_rows = lax.dynamic_slice_in_dim(stream, offset, own_rows, 0)
    inv_rows = lax.dynamic_slice_in_dim(inv_pre, offset, own_rows, 0)
    mlp_out = lax.psum(
        jnp.dot(hidden, w_down, preferred_element_type=jnp.float32), ("mp", "latent")
    )
    grad_output, grad_mlp = output_grads(
        stream, mlp_out, answer_ids, unembed, post_gain, final_gain
    )
    grad_hidden = contract_last(grad_mlp, w_down)
    grad_rows_out = lax.dynamic_slice_in_dim(grad_output, offset, own_rows, 0)
    grad_gate = (grad_hidden * up_proj * gelu_slope(gate_pre)).astype(jnp.bfloat16)
    grad_up = (grad_hidden * activated).astype(jnp.bfloat16)
    grad_normed = lax.psum_scatter(
        contract_last(grad_gate, w_gate) + contract_last(grad_up, w_up),
        ("mp", "latent"),
        scatter_dimension=0,
        tiled=True,
    )
    pre_grad = pre_gain * grad_normed
    grad_stream = (
        grad_rows_out
        + inv_rows * pre_grad
        - stream_rows
        * (inv_rows * inv_rows * inv_rows)
        * jnp.mean(pre_grad * stream_rows, axis=-1, keepdims=True)
    ).astype(jnp.bfloat16)
    clean_code = jax.nn.relu(jnp.dot(clean_all, w_enc, preferred_element_type=jnp.float32) + b_enc)
    corrupt_code = jax.nn.relu(
        jnp.dot(corrupt_all, w_enc, preferred_element_type=jnp.float32) + b_enc
    )
    change = clean_code - corrupt_code
    projected = contract_last(
        lax.all_gather(grad_stream, ("mp", "latent"), axis=0, tiled=True), w_dec
    )
    product = change * projected
    return jnp.sum(product.reshape(total_rows // SEQ, SEQ, product.shape[1]), axis=1)


MESH = pl.DeviceIdType.MESH
BF = jnp.bfloat16
F32 = jnp.float32


PARTS = 3
LANES = 128


class Place:
    def __init__(self, depth):
        self.depth = depth
        self.mp = lax.axis_index("mp")
        self.lat = lax.axis_index("latent")
        self.c, self.y = self.mp % 2, self.mp // 2
        self.x, self.z = self.lat % 2, self.lat // 2
        mp_y, lat_x = (1 - self.y) * 2 + self.c, self.z * 2 + 1 - self.x
        self.core_peer = (self.y * 2 + 1 - self.c, self.lat)
        self.flat_peers = [(self.mp, lat_x), (mp_y, self.lat), (mp_y, lat_x)]
        x, y = self.x, self.y
        self.flat_blocks = [y * 2 + 1 - x, (1 - y) * 2 + x, (1 - y) * 2 + 1 - x]
        self.block = y * 2 + x

    def z_peer(self, step):
        return (self.mp, ((self.z + step) % self.depth) * 2 + self.x)

    def peers(self):
        return [self.core_peer] + self.flat_peers + [self.z_peer(step) for step in range(1, self.depth)]

    def greet(self):
        barrier = pltpu.get_barrier_semaphore()
        for peer in self.peers():
            pl.semaphore_signal(barrier, inc=1, device_id=peer, device_id_type=MESH)

    def meet(self):
        pl.semaphore_wait(pltpu.get_barrier_semaphore(), len(self.peers()))


class Wires:
    def __init__(self, send, recv):
        self.send, self.recv, self.used = send, recv, 0

    def start(self, src, dst, peer):
        i = self.used
        self.used += 1
        copy = pltpu.make_async_remote_copy(
            src_ref=src, dst_ref=dst, send_sem=self.send.at[i], recv_sem=self.recv.at[i],
            device_id=peer, device_id_type=MESH,
        )
        copy.start()
        return copy


def finish(copies):
    for copy in copies:
        copy.wait()


def rows16(start):
    return pl.ds(pl.multiple_of(start, 16), 16)


def rows64(start):
    return pl.ds(pl.multiple_of(start, 64), 64)


def fold(value, depth, row=0):
    width = value.shape[1] // depth
    tokens = 16 // depth
    return jnp.concatenate(
        [value[row : row + tokens, s * width : (s + 1) * width] for s in range(depth)], axis=0
    )


def unfold(blocks, depth):
    tokens = 16 // depth
    return [
        jnp.concatenate([block[s * tokens : (s + 1) * tokens] for block in blocks], axis=0) for s in range(depth)
    ]


class Gather:
    def __init__(self, at, wires, zin, buf, base):
        self.at, self.wires, self.zin, self.buf, self.base = at, wires, zin, buf, base
        self.fine = zin.shape[2] // PARTS
        self.wide = buf.shape[1] // PARTS

    def start(self):
        at, fine = self.at, self.fine
        self.deep = []
        for k in range(PARTS):
            spot = self.zin.at[at.z, :, pl.ds(k * fine, fine)]
            self.deep.append([self.wires.start(spot, spot, at.z_peer(s)) for s in range(1, at.depth)])
        self.flat, self.core = [], []

    def relay(self, k):
        at, fine, wide = self.at, self.fine, self.wide
        finish(self.deep[k])
        blocks = [self.zin[z, :, k * fine : (k + 1) * fine].astype(F32) for z in range(at.depth)]
        mine = rows16(self.base + at.c * 64 + at.block * 16)
        for s, value in enumerate(unfold(blocks, at.depth)):
            self.buf[mine, k * wide + s * fine : k * wide + (s + 1) * fine] = value.astype(BF)
        spot = self.buf.at[mine, pl.ds(k * wide, wide)]
        self.flat.append([self.wires.start(spot, spot, peer) for peer in at.flat_peers])

    def across(self, k):
        finish(self.flat[k])
        spot = self.buf.at[rows64(self.base + self.at.c * 64), pl.ds(k * self.wide, self.wide)]
        self.core.append(self.wires.start(spot, spot, self.at.core_peer))

    def close(self, k):
        finish([self.core[k]])


class Scatter:
    def __init__(self, at, wires, part, bufs, total):
        self.at, self.wires, self.part, self.total = at, wires, part, total
        self.rc, self.s1, self.rf, self.kept, self.sent, self.rz = bufs
        self.wide = part.shape[1] // PARTS
        self.fine = total.shape[1] // PARTS
        self.core, self.flat, self.deep = [], [], []

    def start(self, k):
        span = pl.ds(k * self.wide, self.wide)
        peer = rows64((1 - self.at.c) * 64)
        self.core.append(self.wires.start(self.part.at[peer, span], self.rc.at[:, span], self.at.core_peer))

    def pair(self, k):
        at, wide = self.at, self.wide
        span = pl.ds(k * wide, wide)
        finish([self.core[k]])
        for b in range(4):
            rows = rows16(at.c * 64 + b * 16)
            here = slice(b * 16, b * 16 + 16)
            self.s1[here, span] = (self.part[rows, span].astype(F32) + self.rc[here, span].astype(F32)).astype(BF)
        self.flat.append([
            self.wires.start(self.s1.at[rows16(block * 16), span], self.rf.at[i, :, span], peer)
            for i, (block, peer) in enumerate(zip(at.flat_blocks, at.flat_peers))
        ])

    def settle(self, k):
        at, wide, fine = self.at, self.wide, self.fine
        span = pl.ds(k * wide, wide)
        slot = pl.ds(k * fine, fine)
        finish(self.flat[k])
        value = self.s1[rows16(at.block * 16), span].astype(F32)
        for i in range(3):
            value = value + self.rf[i, :, span].astype(F32)
        for z in range(at.depth):
            piece = fold(value, at.depth, z * (16 // at.depth))
            self.kept[z, :, slot] = piece
            self.sent[z, :, slot] = piece.astype(BF)
        self.deep.append([
            self.wires.start(self.sent.at[(at.z + s) % at.depth, :, slot], self.rz.at[s - 1, :, slot], at.z_peer(s))
            for s in range(1, at.depth)
        ])

    def close(self, k):
        slot = pl.ds(k * self.fine, self.fine)
        finish(self.deep[k])
        value = self.kept[self.at.z, :, slot]
        for s in range(1, self.at.depth):
            value = value + self.rz[s - 1, :, slot].astype(F32)
        self.total[:, slot] = value


def scatter_buffers(d, depth):
    width = d // depth
    return [
        pltpu.VMEM((64, d), BF), pltpu.VMEM((64, d), BF), pltpu.VMEM((3, 16, d), BF),
        pltpu.VMEM((depth, 16, width), F32), pltpu.VMEM((depth, 16, width), BF),
        pltpu.VMEM((depth - 1, 16, width), BF),
    ]


def token_sum(value, depth):
    tokens = 16 // depth
    piece = jnp.broadcast_to(jnp.sum(value, axis=-1, keepdims=True), (16, LANES))
    result = piece
    for s in range(1, depth):
        result = result + pltpu.roll(piece, s * tokens, 0)
    return result[:, 0:1]


def whole_kernel(
    depth, clean, corrupt, answers, unembed_hbm, pre_hbm, post_hbm, final_hbm, wg_hbm, wu_hbm, wd_hbm, we_hbm, be_hbm, wl_hbm, out,
    send, recv, load, wgu, wd, we, wl, unembed, pre_gain, post_gain, final_gain, b_enc, zclean, zcorrupt, zgrad, xs, normed, gu, hidden, gcat,
    part, grads, change, projected, total, stream, pre_f, post_f, weighted, kept, *bufs,
):
    d, both = wgu.shape
    units = both // 2
    latents = out.shape[1]
    rows = normed.shape[0]
    wide, fine = d // PARTS, d // depth // PARTS
    own_rows = clean.shape[0]
    tile = we.shape[2]
    first = latents // 2
    count = latents // tile
    loads = [
        pltpu.make_async_copy(wg_hbm, wgu.at[:, 0:units], load.at[0]),
        pltpu.make_async_copy(wu_hbm, wgu.at[:, units:both], load.at[1]),
        pltpu.make_async_copy(wd_hbm, wd, load.at[2]),
        pltpu.make_async_copy(unembed_hbm, unembed, load.at[3]),
        pltpu.make_async_copy(wl_hbm.at[first:latents], wl, load.at[4]),
    ]
    low = pltpu.make_async_copy(wl_hbm.at[0:first], wd.at[0:first], load.at[5])
    gains = (pre_gain, post_gain, final_gain)
    small = [
        pltpu.make_async_copy(source, gains[i].at[0], load.at[8 + i])
        for i, source in enumerate((pre_hbm, post_hbm, final_hbm))
    ] + [pltpu.make_async_copy(be_hbm, b_enc.at[0], load.at[11])]

    def piece(p):
        return pltpu.make_async_copy(we_hbm.at[:, p * tile : (p + 1) * tile], we.at[p % 2], load.at[6 + p % 2])

    at = Place(depth)
    at.greet()
    for copy in small:
        copy.start()
    for copy in loads[:4]:
        copy.start()
    clean_rows, corrupt_rows = clean[...].astype(F32), corrupt[...].astype(F32)
    for k in range(PARTS):
        span, slot = slice(k * wide, (k + 1) * wide), slice(k * fine, (k + 1) * fine)
        value = fold(clean_rows[:, span], depth)
        stream[:, slot] = value
        zclean[at.z, :, slot] = value.astype(BF)
        zcorrupt[at.z, :, slot] = fold(corrupt_rows[:, span], depth).astype(BF)
    at.meet()
    wires = Wires(send, recv)
    first_rows = Gather(at, wires, zclean, xs, 0)
    other_rows = Gather(at, wires, zcorrupt, xs, rows)
    first_rows.start()
    finish(small)
    for k in range(PARTS):
        span, slot = slice(k * wide, (k + 1) * wide), slice(k * fine, (k + 1) * fine)
        for i, place in enumerate((pre_f, post_f, weighted)):
            place[:, slot] = fold(jnp.broadcast_to(gains[i][:, span], (own_rows, wide)), depth)
    first_rows.relay(0)
    first_rows.relay(1)
    first_rows.relay(2)
    first_rows.across(0)
    piece(0).start()
    piece(1).start()
    loads[4].start()
    first_rows.across(1)
    first_rows.close(0)
    first_rows.across(2)
    other_rows.start()
    first_rows.close(1)
    first_rows.close(2)

    @pl.loop(0, rows // 16)
    def _(i):
        span = rows16(i * 16)
        value = xs[span, :].astype(F32)
        inv_pre = lax.rsqrt(jnp.sum(value * value, axis=-1, keepdims=True) * (1.0 / d) + epsilon)
        normed[span, :] = (value * inv_pre * pre_gain[...]).astype(BF)

    loads[0].wait()
    loads[1].wait()
    cuts = [(a, min(a + 256, units)) for a in range(0, units, 256)]
    for n, (a, b) in enumerate(cuts):
        gate = jnp.dot(normed[...], wgu[:, a:b], preferred_element_type=F32)
        lift = jnp.dot(normed[...], wgu[:, units + a : units + b], preferred_element_type=F32)
        gu[:, a:b] = gate
        gu[:, units + a : units + b] = lift
        hidden[:, a:b] = (gelu_tanh(gate) * lift).astype(BF)
    loads[2].wait()

    def forward(k):
        for a in range(k * wide, (k + 1) * wide, 512):
            part[:, a : a + 512] = jnp.dot(hidden[...], wd[:, a : a + 512], preferred_element_type=F32).astype(BF)

    def backward(k):
        for a in range(k * wide, (k + 1) * wide, 512):
            part[:, a : a + 512] = contract_last(gcat[...], wgu[a : a + 512, :]).astype(BF)

    def aim():
        loads[3].wait()
        base = (at.mp * (2 * depth) + at.lat) * own_rows
        candidate = lax.broadcasted_iota(jnp.int32, (unembed.shape[0], rows), 0)
        selector = (
            jnp.where(candidate == answers[0:1, :], 1.0, 0.0) - jnp.where(candidate == answers[1:2, :], 1.0, 0.0)
        ).astype(BF)
        token = lax.broadcasted_iota(jnp.int32, (rows, 16), 0)
        lane = lax.broadcasted_iota(jnp.int32, (rows, 16), 1)
        pick = jnp.where(token == base + lane % own_rows, 1.0, 0.0).astype(BF)
        chosen = jnp.dot(selector, pick, preferred_element_type=F32).astype(BF)
        for k in range(PARTS):
            value = lax.dot_general(
                chosen, unembed[:, k * wide : (k + 1) * wide], (((0,), (0,)), ((), ())), preferred_element_type=F32
            )
            slot = slice(k * fine, (k + 1) * fine)
            weighted[:, slot] = weighted[:, slot] * fold(value, depth)

    def slopes():
        for a, b in cuts:
            gate, lift = gu[:, a:b], gu[:, units + a : units + b]
            gu[:, a:b] = lift * gelu_slope(gate)
            gu[:, units + a : units + b] = gelu_tanh(gate)

    def encode():
        for p in range(count):
            piece(p).wait()
            span = slice(p * tile, (p + 1) * tile)
            code = jnp.dot(xs[...], we[p % 2], preferred_element_type=F32) + b_enc[:, span]
            code = jnp.maximum(code, 0.0)
            change[:, span] = code[:rows] - code[rows:]
            if p + 2 < count:
                piece(p + 2).start()
            yield

    def turn():
        loads[4].wait()
        low.wait()
        for p in range(count):
            source = wd if (p + 1) * tile <= first else wl
            base = p * tile % first
            wgu[:, p * tile : (p + 1) * tile] = source[base : base + tile, :].T
            yield

    work = itertools.chain(encode(), turn())

    def fill(n):
        for _ in range(n):
            next(work, None)

    def scatter(produce, plan):
        run = Scatter(at, wires, part, bufs, total)
        for k in range(PARTS):
            produce(k)
            run.start(k)
            if k > 0:
                run.pair(k - 1)
        run.pair(PARTS - 1)
        plan(0)
        for k in range(PARTS):
            run.settle(k)
            plan(k + 1)
        for k in range(PARTS):
            run.close(k)

    def gather(zin, use, plan, ahead=lambda: None):
        run = Gather(at, wires, zin, grads, 0)
        run.start()
        ahead()
        for k in range(PARTS):
            run.relay(k)
        plan()
        run.across(0)
        for k in range(PARTS):
            run.close(k)
            for n, _ in enumerate(use(k)):
                if n == 0 and k + 1 < PARTS:
                    run.across(k + 1)

    def plan(k):
        if k == 0:
            slopes()
            aim()
        elif k == PARTS:
            for i in range(PARTS):
                other_rows.relay(i)

    scatter(forward, plan)
    m, s, pg, wt = total[...], stream[...], post_f[...], weighted[...]
    mg = m * pg
    mean = lambda value: token_sum(value, depth) * (1.0 / d)
    mm, ss, smg, mgmg, ws, wmg = mean(m * m), mean(s * s), mean(s * mg), mean(mg * mg), mean(wt * s), mean(wt * mg)
    inv_post = lax.rsqrt(mm + epsilon)
    inv_final = lax.rsqrt(ss + 2.0 * inv_post * smg + inv_post * inv_post * mgmg + epsilon)
    output = s + mg * inv_post
    lean = (inv_final * inv_final * inv_final) * (ws + inv_post * wmg)
    grad_output = inv_final * wt - output * lean
    pull = inv_final * wmg - lean * (smg + inv_post * mgmg)
    grad_mlp = inv_post * (pg * grad_output) - m * (inv_post * inv_post * inv_post) * pull
    kept[...] = grad_output
    zgrad[at.z] = grad_mlp.astype(BF)

    def hidden_grad(k):
        span = slice(k * wide, (k + 1) * wide)
        for n, (a, b) in enumerate(cuts):
            if n == len(cuts) // 2:
                yield
            value = contract_last(grads[:, span], wd[a:b, span])
            if k > 0:
                value = value + projected[:, a:b]
            if k + 1 < PARTS:
                projected[:, a:b] = value
            else:
                gcat[:, a:b] = (value * gu[:, a:b]).astype(BF)
                gcat[:, units + a : units + b] = (value * gu[:, units + a : units + b]).astype(BF)

    def meanwhile():
        for k in range(PARTS):
            other_rows.across(k)

    gather(zgrad, hidden_grad, meanwhile)
    for k in range(PARTS):
        other_rows.close(k)
    low.start()
    scatter(backward, lambda k: fill((1, 2, 2, 3)[k]))
    pre_grad = pre_f[...] * total[...]
    s = stream[...]
    inv_pre = lax.rsqrt(mean(s * s) + epsilon)
    lean = (inv_pre * inv_pre * inv_pre) * mean(pre_grad * s)
    zgrad[at.z] = (kept[...] + inv_pre * pre_grad - s * lean).astype(BF)

    def decode(k):
        span = slice(k * wide, (k + 1) * wide)
        step = 512
        for a in range(0, latents, step):
            if a == latents // 2:
                yield
            value = jnp.dot(grads[:, span], wgu[span, a : a + step], preferred_element_type=F32)
            if k > 0:
                value = value + projected[:, a : a + step]
            if k + 1 < PARTS:
                projected[:, a : a + step] = value
            else:
                out[:, a : a + step] = jnp.sum(change[:, a : a + step] * value, axis=0, keepdims=True)

    gather(zgrad, decode, lambda: fill(2 * count), lambda: fill(3))


def staged(
    depth,
    resid_clean,
    resid_corrupt,
    answer_ids,
    unembed,
    pre_gain,
    post_gain,
    final_gain,
    w_gate,
    w_up,
    w_down,
    w_enc,
    b_enc,
    w_dec,
):
    own_rows, d = resid_clean.shape
    width = d // depth
    units = w_gate.shape[1]
    latents = w_enc.shape[1]
    rows = own_rows * depth * 8
    tile = 256
    vmem = pl.BlockSpec(memory_space=pltpu.VMEM)
    hbm = pl.BlockSpec(memory_space=pl.ANY)
    scratch = [
        pltpu.SemaphoreType.DMA((128,)), pltpu.SemaphoreType.DMA((128,)), pltpu.SemaphoreType.DMA((12,)),
        pltpu.VMEM((d, 2 * units), BF), pltpu.VMEM((units, d), BF),
        pltpu.VMEM((2, d, tile), BF), pltpu.VMEM((latents // 2, d), BF), pltpu.VMEM(unembed.shape, BF),
        pltpu.VMEM((1, d), F32), pltpu.VMEM((1, d), F32), pltpu.VMEM((1, d), F32), pltpu.VMEM((1, latents), F32),
        pltpu.VMEM((depth, 16, width), BF), pltpu.VMEM((depth, 16, width), BF), pltpu.VMEM((depth, 16, width), BF),
        pltpu.VMEM((2 * rows, d), BF), pltpu.VMEM((rows, d), BF),
        pltpu.VMEM((rows, 2 * units), F32), pltpu.VMEM((rows, units), BF), pltpu.VMEM((rows, 2 * units), BF),
        pltpu.VMEM((rows, d), BF), pltpu.VMEM((rows, d), BF), pltpu.VMEM((rows, latents), F32),
        pltpu.VMEM((rows, latents), F32),
    ] + [pltpu.VMEM((16, width), F32)] * 6 + scatter_buffers(d, depth)
    return pl.pallas_call(
        functools.partial(whole_kernel, depth),
        out_shape=jax.ShapeDtypeStruct((1, latents), F32),
        in_specs=[vmem] * 3 + [hbm] * 10,
        out_specs=vmem,
        scratch_shapes=scratch,
        compiler_params=pltpu.CompilerParams(
            collective_id=0, has_side_effects=True, vmem_limit_bytes=67043328
        ),
    )(
        resid_clean, resid_corrupt, answer_ids.T, unembed, pre_gain, post_gain, final_gain,
        w_gate, w_up, w_down, w_enc, b_enc, w_dec,
    )


def fits(mesh, own_rows, d, units, latents, candidates):
    depth = mesh.shape["latent"] // 2
    rows = own_rows * mesh.shape["mp"] * mesh.shape["latent"]
    return (
        mesh.shape["mp"] == 4 and depth in (2, 4) and own_rows * depth == 16 and rows == SEQ
        and d % (128 * depth * PARTS) == 0 and d % (512 * PARTS) == 0 and candidates % 128 == 0
        and units % 128 == 0 and latents % 1024 == 0 and latents // 2 <= units
    )


def solution(mesh):
    def chosen(resid_clean, *rest):
        own_rows, d = resid_clean.shape
        if fits(mesh, own_rows, d, rest[6].shape[1], rest[9].shape[1], rest[2].shape[0]):
            return staged(mesh.shape["latent"] // 2, resid_clean, *rest)
        return local(resid_clean, *rest)

    return jax.shard_map(
        chosen,
        mesh=mesh,
        in_specs=(
            P(("mp", "latent"), None),
            P(("mp", "latent"), None),
            P(),
            P(),
            P(),
            P(),
            P(),
            P(None, ("mp", "latent")),
            P(None, ("mp", "latent")),
            P(("mp", "latent"), None),
            P(None, ("mp", "latent")),
            P(("mp", "latent")),
            P(("mp", "latent"), None),
        ),
        out_specs=P(None, ("mp", "latent")),
        check_vma=False,
    )
```

```python
import functools
import itertools

import jax
import jax.numpy as jnp
from jax import lax
from jax.experimental import pallas as pl
from jax.experimental.pallas import tpu as pltpu
from jax.sharding import PartitionSpec as P

SEQ = 128


epsilon = 1e-06
gelu_scale = 0.7978845608028654
gelu_cubic = 0.044715


def gelu_tanh(value):
    return 0.5 * value * (1.0 + jnp.tanh(gelu_scale * (value + gelu_cubic * value * value * value)))


def gelu_slope(value):
    inner = jnp.tanh(gelu_scale * (value + gelu_cubic * value * value * value))
    return 0.5 * (1.0 + inner) + 0.5 * value * (1.0 - inner * inner) * gelu_scale * (
        1.0 + 3.0 * gelu_cubic * value * value
    )


def contract_last(left, right):
    return lax.dot_general(
        left, right, (((1,), (1,)), ((), ())), preferred_element_type=jnp.float32
    )


def output_grads(stream, mlp_out, answers, unembed, post_gain, final_gain):
    inv_post = lax.rsqrt(jnp.mean(mlp_out * mlp_out, axis=-1, keepdims=True) + epsilon)
    output = stream + mlp_out * inv_post * post_gain
    inv_final = lax.rsqrt(jnp.mean(output * output, axis=-1, keepdims=True) + epsilon)
    candidate = lax.broadcasted_iota(jnp.int32, (answers.shape[0], unembed.shape[0]), 1)
    selector = (
        (candidate == answers[:, 0:1]).astype(jnp.float32)
        - (candidate == answers[:, 1:2]).astype(jnp.float32)
    ).astype(jnp.bfloat16)
    direction = jnp.dot(selector, unembed, preferred_element_type=jnp.float32)
    weighted = final_gain * direction
    grad_output = inv_final * weighted - output * (inv_final * inv_final * inv_final) * jnp.mean(
        weighted * output, axis=-1, keepdims=True
    )
    post_grad = post_gain * grad_output
    grad_mlp = (
        inv_post * post_grad
        - mlp_out
        * (inv_post * inv_post * inv_post)
        * jnp.mean(post_grad * mlp_out, axis=-1, keepdims=True)
    ).astype(jnp.bfloat16)
    return (grad_output, grad_mlp)


def local(
    resid_clean,
    resid_corrupt,
    answer_ids,
    unembed,
    pre_gain,
    post_gain,
    final_gain,
    w_gate,
    w_up,
    w_down,
    w_enc,
    b_enc,
    w_dec,
):
    own_rows = resid_clean.shape[0]
    clean_all, corrupt_all = (
        lax.all_gather(resid_clean, ("mp", "latent"), axis=0, tiled=True),
        lax.all_gather(resid_corrupt, ("mp", "latent"), axis=0, tiled=True),
    )
    total_rows = clean_all.shape[0]
    offset = lax.axis_index(("mp", "latent")) * own_rows
    stream = clean_all.astype(jnp.float32)
    inv_pre = lax.rsqrt(jnp.mean(stream * stream, axis=-1, keepdims=True) + epsilon)
    normed = (stream * inv_pre * pre_gain).astype(jnp.bfloat16)
    gate_pre = jnp.dot(normed, w_gate, preferred_element_type=jnp.float32)
    up_proj = jnp.dot(normed, w_up, preferred_element_type=jnp.float32)
    activated = gelu_tanh(gate_pre)
    hidden = (activated * up_proj).astype(jnp.bfloat16)
    stream_rows = lax.dynamic_slice_in_dim(stream, offset, own_rows, 0)
    inv_rows = lax.dynamic_slice_in_dim(inv_pre, offset, own_rows, 0)
    mlp_out = lax.psum(
        jnp.dot(hidden, w_down, preferred_element_type=jnp.float32), ("mp", "latent")
    )
    grad_output, grad_mlp = output_grads(
        stream, mlp_out, answer_ids, unembed, post_gain, final_gain
    )
    grad_hidden = contract_last(grad_mlp, w_down)
    grad_rows_out = lax.dynamic_slice_in_dim(grad_output, offset, own_rows, 0)
    grad_gate = (grad_hidden * up_proj * gelu_slope(gate_pre)).astype(jnp.bfloat16)
    grad_up = (grad_hidden * activated).astype(jnp.bfloat16)
    grad_normed = lax.psum_scatter(
        contract_last(grad_gate, w_gate) + contract_last(grad_up, w_up),
        ("mp", "latent"),
        scatter_dimension=0,
        tiled=True,
    )
    pre_grad = pre_gain * grad_normed
    grad_stream = (
        grad_rows_out
        + inv_rows * pre_grad
        - stream_rows
        * (inv_rows * inv_rows * inv_rows)
        * jnp.mean(pre_grad * stream_rows, axis=-1, keepdims=True)
    ).astype(jnp.bfloat16)
    clean_code = jax.nn.relu(jnp.dot(clean_all, w_enc, preferred_element_type=jnp.float32) + b_enc)
    corrupt_code = jax.nn.relu(
        jnp.dot(corrupt_all, w_enc, preferred_element_type=jnp.float32) + b_enc
    )
    change = clean_code - corrupt_code
    projected = contract_last(
        lax.all_gather(grad_stream, ("mp", "latent"), axis=0, tiled=True), w_dec
    )
    product = change * projected
    return jnp.sum(product.reshape(total_rows // SEQ, SEQ, product.shape[1]), axis=1)


MESH = pl.DeviceIdType.MESH
BF = jnp.bfloat16
F32 = jnp.float32


PARTS = 3
LANES = 128


class Place:
    def __init__(self, depth):
        self.depth = depth
        self.mp = lax.axis_index("mp")
        self.lat = lax.axis_index("latent")
        self.c, self.y = self.mp % 2, self.mp // 2
        self.x, self.z = self.lat % 2, self.lat // 2
        mp_y, lat_x = (1 - self.y) * 2 + self.c, self.z * 2 + 1 - self.x
        self.core_peer = (self.y * 2 + 1 - self.c, self.lat)
        self.flat_peers = [(mp_y, lat_x), (self.mp, lat_x), (mp_y, self.lat)]
        x, y = self.x, self.y
        self.flat_blocks = [(1 - y) * 2 + 1 - x, y * 2 + 1 - x, (1 - y) * 2 + x]
        self.block = y * 2 + x

    def z_peer(self, step):
        return (self.mp, ((self.z + step) % self.depth) * 2 + self.x)

    def peers(self):
        return [self.core_peer] + self.flat_peers + [self.z_peer(step) for step in range(1, self.depth)]

    def greet(self):
        barrier = pltpu.get_barrier_semaphore()
        for peer in self.peers():
            pl.semaphore_signal(barrier, inc=1, device_id=peer, device_id_type=MESH)

    def meet(self):
        pl.semaphore_wait(pltpu.get_barrier_semaphore(), len(self.peers()))


class Wires:
    def __init__(self, send, recv):
        self.send, self.recv, self.used = send, recv, 0

    def start(self, src, dst, peer):
        i = self.used
        self.used += 1
        copy = pltpu.make_async_remote_copy(
            src_ref=src, dst_ref=dst, send_sem=self.send.at[i], recv_sem=self.recv.at[i],
            device_id=peer, device_id_type=MESH,
        )
        copy.start()
        return copy


def finish(copies):
    for copy in copies:
        copy.wait()


def rows16(start):
    return pl.ds(pl.multiple_of(start, 16), 16)


def rows64(start):
    return pl.ds(pl.multiple_of(start, 64), 64)


def fold(value, depth, row=0):
    width = value.shape[1] // depth
    tokens = 16 // depth
    return jnp.concatenate(
        [value[row : row + tokens, s * width : (s + 1) * width] for s in range(depth)], axis=0
    )


def unfold(blocks, depth):
    tokens = 16 // depth
    return [
        jnp.concatenate([block[s * tokens : (s + 1) * tokens] for block in blocks], axis=0) for s in range(depth)
    ]


class Gather:
    def __init__(self, at, wires, zin, buf, base):
        self.at, self.wires, self.zin, self.buf, self.base = at, wires, zin, buf, base
        self.fine = zin.shape[2] // PARTS
        self.wide = buf.shape[1] // PARTS

    def start(self):
        at, fine = self.at, self.fine
        self.deep = []
        for k in range(PARTS):
            spot = self.zin.at[at.z, :, pl.ds(k * fine, fine)]
            self.deep.append([self.wires.start(spot, spot, at.z_peer(s)) for s in range(1, at.depth)])
        self.flat, self.core = [], []

    def relay(self, k):
        at, fine, wide = self.at, self.fine, self.wide
        finish(self.deep[k])
        blocks = [self.zin[z, :, k * fine : (k + 1) * fine].astype(F32) for z in range(at.depth)]
        mine = rows16(self.base + at.c * 64 + at.block * 16)
        for s, value in enumerate(unfold(blocks, at.depth)):
            self.buf[mine, k * wide + s * fine : k * wide + (s + 1) * fine] = value.astype(BF)
        spot = self.buf.at[mine, pl.ds(k * wide, wide)]
        self.flat.append([self.wires.start(spot, spot, peer) for peer in at.flat_peers])

    def across(self, k):
        finish(self.flat[k])
        spot = self.buf.at[rows64(self.base + self.at.c * 64), pl.ds(k * self.wide, self.wide)]
        self.core.append(self.wires.start(spot, spot, self.at.core_peer))

    def close(self, k):
        finish([self.core[k]])


class Scatter:
    def __init__(self, at, wires, part, bufs, total):
        self.at, self.wires, self.part, self.total = at, wires, part, total
        self.rc, self.s1, self.rf, self.kept, self.sent, self.rz = bufs
        self.wide = part.shape[1] // PARTS
        self.fine = total.shape[1] // PARTS
        self.core, self.flat, self.deep = [], [], []

    def start(self, k):
        span = pl.ds(k * self.wide, self.wide)
        peer = rows64((1 - self.at.c) * 64)
        self.core.append(self.wires.start(self.part.at[peer, span], self.rc.at[:, span], self.at.core_peer))

    def pair(self, k):
        at, wide = self.at, self.wide
        span = pl.ds(k * wide, wide)
        finish([self.core[k]])
        for b in range(4):
            rows = rows16(at.c * 64 + b * 16)
            here = slice(b * 16, b * 16 + 16)
            self.s1[here, span] = (self.part[rows, span].astype(F32) + self.rc[here, span].astype(F32)).astype(BF)
        self.flat.append([
            self.wires.start(self.s1.at[rows16(block * 16), span], self.rf.at[i, :, span], peer)
            for i, (block, peer) in enumerate(zip(at.flat_blocks, at.flat_peers))
        ])

    def settle(self, k):
        at, wide, fine = self.at, self.wide, self.fine
        span = pl.ds(k * wide, wide)
        slot = pl.ds(k * fine, fine)
        finish(self.flat[k])
        value = self.s1[rows16(at.block * 16), span].astype(F32)
        for i in range(3):
            value = value + self.rf[i, :, span].astype(F32)
        for z in range(at.depth):
            piece = fold(value, at.depth, z * (16 // at.depth))
            self.kept[z, :, slot] = piece
            self.sent[z, :, slot] = piece.astype(BF)
        self.deep.append([
            self.wires.start(self.sent.at[(at.z + s) % at.depth, :, slot], self.rz.at[s - 1, :, slot], at.z_peer(s))
            for s in range(1, at.depth)
        ])

    def close(self, k):
        slot = pl.ds(k * self.fine, self.fine)
        finish(self.deep[k])
        value = self.kept[self.at.z, :, slot]
        for s in range(1, self.at.depth):
            value = value + self.rz[s - 1, :, slot].astype(F32)
        self.total[:, slot] = value


def scatter_buffers(d, depth):
    width = d // depth
    return [
        pltpu.VMEM((64, d), BF), pltpu.VMEM((64, d), BF), pltpu.VMEM((3, 16, d), BF),
        pltpu.VMEM((depth, 16, width), F32), pltpu.VMEM((depth, 16, width), BF),
        pltpu.VMEM((depth - 1, 16, width), BF),
    ]


def token_sum(value, depth):
    tokens = 16 // depth
    piece = jnp.broadcast_to(jnp.sum(value, axis=-1, keepdims=True), (16, LANES))
    result = piece
    for s in range(1, depth):
        result = result + pltpu.roll(piece, s * tokens, 0)
    return result[:, 0:1]


def whole_kernel(
    depth, clean, corrupt, answers, unembed_hbm, pre_hbm, post_hbm, final_hbm, wg_hbm, wu_hbm, wd_hbm, we_hbm, be_hbm, wl_hbm, out,
    send, recv, load, wgu, wd, we, wl, unembed, pre_gain, post_gain, final_gain, b_enc, zclean, zcorrupt, zgrad, xs, normed, gu, hidden, gcat,
    part, grads, change, projected, total, stream, pre_f, post_f, weighted, kept, *bufs,
):
    d, both = wgu.shape
    units = both // 2
    latents = out.shape[1]
    rows = normed.shape[0]
    wide, fine = d // PARTS, d // depth // PARTS
    own_rows = clean.shape[0]
    tile = we.shape[2]
    first = latents // 2
    count = latents // tile
    loads = [
        pltpu.make_async_copy(wg_hbm, wgu.at[:, 0:units], load.at[0]),
        pltpu.make_async_copy(wu_hbm, wgu.at[:, units:both], load.at[1]),
        pltpu.make_async_copy(wd_hbm, wd, load.at[2]),
        pltpu.make_async_copy(unembed_hbm, unembed, load.at[3]),
        pltpu.make_async_copy(wl_hbm.at[first:latents], wl, load.at[4]),
    ]
    low = pltpu.make_async_copy(wl_hbm.at[0:first], wd.at[0:first], load.at[5])
    gains = (pre_gain, post_gain, final_gain)
    small = [
        pltpu.make_async_copy(source, gains[i].at[0], load.at[8 + i])
        for i, source in enumerate((pre_hbm, post_hbm, final_hbm))
    ] + [pltpu.make_async_copy(be_hbm, b_enc.at[0], load.at[11])]

    def piece(p):
        return pltpu.make_async_copy(we_hbm.at[:, p * tile : (p + 1) * tile], we.at[p % 2], load.at[6 + p % 2])

    at = Place(depth)
    at.greet()
    for copy in small:
        copy.start()
    for copy in loads[:4]:
        copy.start()
    clean_rows, corrupt_rows = clean[...].astype(F32), corrupt[...].astype(F32)
    for k in range(PARTS):
        span, slot = slice(k * wide, (k + 1) * wide), slice(k * fine, (k + 1) * fine)
        value = fold(clean_rows[:, span], depth)
        stream[:, slot] = value
        zclean[at.z, :, slot] = value.astype(BF)
        zcorrupt[at.z, :, slot] = fold(corrupt_rows[:, span], depth).astype(BF)
    at.meet()
    wires = Wires(send, recv)
    first_rows = Gather(at, wires, zclean, xs, 0)
    other_rows = Gather(at, wires, zcorrupt, xs, rows)
    first_rows.start()
    finish(small)
    for k in range(PARTS):
        span, slot = slice(k * wide, (k + 1) * wide), slice(k * fine, (k + 1) * fine)
        for i, place in enumerate((pre_f, post_f, weighted)):
            place[:, slot] = fold(jnp.broadcast_to(gains[i][:, span], (own_rows, wide)), depth)
    first_rows.relay(0)
    first_rows.relay(1)
    first_rows.relay(2)
    first_rows.across(0)
    piece(0).start()
    piece(1).start()
    loads[4].start()
    first_rows.across(1)
    first_rows.close(0)
    first_rows.across(2)
    other_rows.start()
    first_rows.close(1)
    first_rows.close(2)

    @pl.loop(0, rows // 16)
    def _(i):
        span = rows16(i * 16)
        value = xs[span, :].astype(F32)
        inv_pre = lax.rsqrt(jnp.sum(value * value, axis=-1, keepdims=True) * (1.0 / d) + epsilon)
        normed[span, :] = (value * inv_pre * pre_gain[...]).astype(BF)

    loads[0].wait()
    loads[1].wait()
    cuts = [(a, min(a + 256, units)) for a in range(0, units, 256)]
    for n, (a, b) in enumerate(cuts):
        gate = jnp.dot(normed[...], wgu[:, a:b], preferred_element_type=F32)
        lift = jnp.dot(normed[...], wgu[:, units + a : units + b], preferred_element_type=F32)
        gu[:, a:b] = gate
        gu[:, units + a : units + b] = lift
        hidden[:, a:b] = (gelu_tanh(gate) * lift).astype(BF)
    loads[2].wait()

    def forward(k):
        for a in range(k * wide, (k + 1) * wide, 512):
            part[:, a : a + 512] = jnp.dot(hidden[...], wd[:, a : a + 512], preferred_element_type=F32).astype(BF)

    def backward(k):
        for a in range(k * wide, (k + 1) * wide, 512):
            part[:, a : a + 512] = contract_last(gcat[...], wgu[a : a + 512, :]).astype(BF)

    def aim():
        loads[3].wait()
        base = (at.mp * (2 * depth) + at.lat) * own_rows
        candidate = lax.broadcasted_iota(jnp.int32, (unembed.shape[0], rows), 0)
        selector = (
            jnp.where(candidate == answers[0:1, :], 1.0, 0.0) - jnp.where(candidate == answers[1:2, :], 1.0, 0.0)
        ).astype(BF)
        token = lax.broadcasted_iota(jnp.int32, (rows, 16), 0)
        lane = lax.broadcasted_iota(jnp.int32, (rows, 16), 1)
        pick = jnp.where(token == base + lane % own_rows, 1.0, 0.0).astype(BF)
        chosen = jnp.dot(selector, pick, preferred_element_type=F32).astype(BF)
        for k in range(PARTS):
            value = lax.dot_general(
                chosen, unembed[:, k * wide : (k + 1) * wide], (((0,), (0,)), ((), ())), preferred_element_type=F32
            )
            slot = slice(k * fine, (k + 1) * fine)
            weighted[:, slot] = weighted[:, slot] * fold(value, depth)

    def slopes():
        for a, b in cuts:
            gate, lift = gu[:, a:b], gu[:, units + a : units + b]
            gu[:, a:b] = lift * gelu_slope(gate)
            gu[:, units + a : units + b] = gelu_tanh(gate)

    def encode():
        for p in range(count):
            piece(p).wait()
            span = slice(p * tile, (p + 1) * tile)
            code = jnp.dot(xs[...], we[p % 2], preferred_element_type=F32) + b_enc[:, span]
            code = jnp.maximum(code, 0.0)
            change[:, span] = code[:rows] - code[rows:]
            if p + 2 < count:
                piece(p + 2).start()
            yield

    def turn():
        loads[4].wait()
        low.wait()
        for p in range(count):
            source = wd if (p + 1) * tile <= first else wl
            base = p * tile % first
            wgu[:, p * tile : (p + 1) * tile] = source[base : base + tile, :].T
            yield

    work = itertools.chain(encode(), turn())

    def fill(n):
        for _ in range(n):
            next(work, None)

    def scatter(produce, plan):
        run = Scatter(at, wires, part, bufs, total)
        for k in range(PARTS):
            produce(k)
            run.start(k)
            if k > 0:
                run.pair(k - 1)
        run.pair(PARTS - 1)
        plan(0)
        for k in range(PARTS):
            run.settle(k)
            plan(k + 1)
        for k in range(PARTS):
            run.close(k)

    def gather(zin, use, plan, ahead=lambda: None):
        run = Gather(at, wires, zin, grads, 0)
        run.start()
        ahead()
        for k in range(PARTS):
            run.relay(k)
        plan()
        run.across(0)
        for k in range(PARTS):
            run.close(k)
            for n, _ in enumerate(use(k)):
                if n == 0 and k + 1 < PARTS:
                    run.across(k + 1)

    def plan(k):
        if k == 0:
            slopes()
            aim()
        elif k == PARTS:
            for i in range(PARTS):
                other_rows.relay(i)

    scatter(forward, plan)
    m, s, pg, wt = total[...], stream[...], post_f[...], weighted[...]
    mg = m * pg
    mean = lambda value: token_sum(value, depth) * (1.0 / d)
    mm, ss, smg, mgmg, ws, wmg = mean(m * m), mean(s * s), mean(s * mg), mean(mg * mg), mean(wt * s), mean(wt * mg)
    inv_post = lax.rsqrt(mm + epsilon)
    inv_final = lax.rsqrt(ss + 2.0 * inv_post * smg + inv_post * inv_post * mgmg + epsilon)
    output = s + mg * inv_post
    lean = (inv_final * inv_final * inv_final) * (ws + inv_post * wmg)
    grad_output = inv_final * wt - output * lean
    pull = inv_final * wmg - lean * (smg + inv_post * mgmg)
    grad_mlp = inv_post * (pg * grad_output) - m * (inv_post * inv_post * inv_post) * pull
    kept[...] = grad_output
    zgrad[at.z] = grad_mlp.astype(BF)

    def hidden_grad(k):
        span = slice(k * wide, (k + 1) * wide)
        for n, (a, b) in enumerate(cuts):
            if n == len(cuts) // 2:
                yield
            value = contract_last(grads[:, span], wd[a:b, span])
            if k > 0:
                value = value + projected[:, a:b]
            if k + 1 < PARTS:
                projected[:, a:b] = value
            else:
                gcat[:, a:b] = (value * gu[:, a:b]).astype(BF)
                gcat[:, units + a : units + b] = (value * gu[:, units + a : units + b]).astype(BF)

    def meanwhile():
        for k in range(PARTS):
            other_rows.across(k)

    gather(zgrad, hidden_grad, meanwhile)
    for k in range(PARTS):
        other_rows.close(k)
    low.start()
    scatter(backward, lambda k: fill((1, 2, 2, 3)[k]))
    pre_grad = pre_f[...] * total[...]
    s = stream[...]
    inv_pre = lax.rsqrt(mean(s * s) + epsilon)
    lean = (inv_pre * inv_pre * inv_pre) * mean(pre_grad * s)
    zgrad[at.z] = (kept[...] + inv_pre * pre_grad - s * lean).astype(BF)

    def decode(k):
        span = slice(k * wide, (k + 1) * wide)
        step = 512
        for a in range(0, latents, step):
            if a == latents // 2:
                yield
            value = jnp.dot(grads[:, span], wgu[span, a : a + step], preferred_element_type=F32)
            if k > 0:
                value = value + projected[:, a : a + step]
            if k + 1 < PARTS:
                projected[:, a : a + step] = value
            else:
                out[:, a : a + step] = jnp.sum(change[:, a : a + step] * value, axis=0, keepdims=True)

    gather(zgrad, decode, lambda: fill(2 * count), lambda: fill(3))


def staged(
    depth,
    resid_clean,
    resid_corrupt,
    answer_ids,
    unembed,
    pre_gain,
    post_gain,
    final_gain,
    w_gate,
    w_up,
    w_down,
    w_enc,
    b_enc,
    w_dec,
):
    own_rows, d = resid_clean.shape
    width = d // depth
    units = w_gate.shape[1]
    latents = w_enc.shape[1]
    rows = own_rows * depth * 8
    tile = 256
    vmem = pl.BlockSpec(memory_space=pltpu.VMEM)
    hbm = pl.BlockSpec(memory_space=pl.ANY)
    scratch = [
        pltpu.SemaphoreType.DMA((128,)), pltpu.SemaphoreType.DMA((128,)), pltpu.SemaphoreType.DMA((12,)),
        pltpu.VMEM((d, 2 * units), BF), pltpu.VMEM((units, d), BF),
        pltpu.VMEM((2, d, tile), BF), pltpu.VMEM((latents // 2, d), BF), pltpu.VMEM(unembed.shape, BF),
        pltpu.VMEM((1, d), F32), pltpu.VMEM((1, d), F32), pltpu.VMEM((1, d), F32), pltpu.VMEM((1, latents), F32),
        pltpu.VMEM((depth, 16, width), BF), pltpu.VMEM((depth, 16, width), BF), pltpu.VMEM((depth, 16, width), BF),
        pltpu.VMEM((2 * rows, d), BF), pltpu.VMEM((rows, d), BF),
        pltpu.VMEM((rows, 2 * units), F32), pltpu.VMEM((rows, units), BF), pltpu.VMEM((rows, 2 * units), BF),
        pltpu.VMEM((rows, d), BF), pltpu.VMEM((rows, d), BF), pltpu.VMEM((rows, latents), F32),
        pltpu.VMEM((rows, latents), F32),
    ] + [pltpu.VMEM((16, width), F32)] * 6 + scatter_buffers(d, depth)
    return pl.pallas_call(
        functools.partial(whole_kernel, depth),
        out_shape=jax.ShapeDtypeStruct((1, latents), F32),
        in_specs=[vmem] * 3 + [hbm] * 10,
        out_specs=vmem,
        scratch_shapes=scratch,
        compiler_params=pltpu.CompilerParams(
            collective_id=0, has_side_effects=True, vmem_limit_bytes=67043328
        ),
    )(
        resid_clean, resid_corrupt, answer_ids.T, unembed, pre_gain, post_gain, final_gain,
        w_gate, w_up, w_down, w_enc, b_enc, w_dec,
    )


def fits(mesh, own_rows, d, units, latents, candidates):
    depth = mesh.shape["latent"] // 2
    rows = own_rows * mesh.shape["mp"] * mesh.shape["latent"]
    return (
        mesh.shape["mp"] == 4 and depth in (2, 4) and own_rows * depth == 16 and rows == SEQ
        and d % (128 * depth * PARTS) == 0 and d % (512 * PARTS) == 0 and candidates % 128 == 0
        and units % 128 == 0 and latents % 1024 == 0 and latents // 2 <= units
    )


def solution(mesh):
    def chosen(resid_clean, *rest):
        own_rows, d = resid_clean.shape
        if fits(mesh, own_rows, d, rest[6].shape[1], rest[9].shape[1], rest[2].shape[0]):
            return staged(mesh.shape["latent"] // 2, resid_clean, *rest)
        return local(resid_clean, *rest)

    return jax.shard_map(
        chosen,
        mesh=mesh,
        in_specs=(
            P(("mp", "latent"), None),
            P(("mp", "latent"), None),
            P(),
            P(),
            P(),
            P(),
            P(),
            P(None, ("mp", "latent")),
            P(None, ("mp", "latent")),
            P(("mp", "latent"), None),
            P(None, ("mp", "latent")),
            P(("mp", "latent")),
            P(("mp", "latent"), None),
        ),
        out_specs=P(None, ("mp", "latent")),
        check_vma=False,
    )
```
